32 devices in a mesh: section: 2 (over core), seq: 4 (over y, x), wshard: 4 (over z).
Axes of the slice: x: 2, y: 2, z: 4, core: 2. Of those that a mesh axis runs over, the one named last changes fastest.
Arguments:
- boundary: bfloat16 [2, 4, 2, 768, 1152], P('section', 'wshard', None, 'seq'), may hold values from -6 to 6
- seq_lengths: int32 [4], P('wshard'), may hold values from 768 to 1536, as said below
- heads_weight: bfloat16 [2, 1152, 1536], P('section', 'wshard'), may hold values from -0.1875 to 0.1875
- merge_weight: bfloat16 [2, 1024, 1152], P('section', 'wshard'), may hold values from -0.1875 to 0.1875
- gate_weight: bfloat16 [2, 1152, 6912], P('section', None, 'wshard'), may hold values from -0.1875 to 0.1875
- up_weight: bfloat16 [2, 1152, 6912], P('section', None, 'wshard'), may hold values from -0.1875 to 0.1875
- down_weight: bfloat16 [2, 6912, 1152], P('section', 'wshard'), may hold values from -0.078125 to 0.078125
- norm_gains: float32 [2, 5120], P('section'), may hold values from 0.5 to 1.5
Outputs:
- activations: bfloat16 [2, 4, 2, 768, 1152], P('section', 'wshard', None, 'seq')
- boundary_grads: bfloat16 [2, 4, 2, 768, 1152], P('section', 'wshard', None, 'seq')
- heads_gradient: float32 [2, 1152, 1536], P('section', ('seq', 'wshard'))
- merge_gradient: float32 [2, 1024, 1152], P('section', ('seq', 'wshard'))
- gate_gradient: float32 [2, 1152, 6912], P('section', None, ('seq', 'wshard'))
- up_gradient: float32 [2, 1152, 6912], P('section', None, ('seq', 'wshard'))
- down_gradient: float32 [2, 6912, 1152], P('section', ('seq', 'wshard'))
- gains_gradient: float32 [2, 5120], P('section', ('seq', 'wshard'))
The draws below stay inside these ranges and needn't reach their ends.
Inputs may be any that keep to these rules, and one draw needn't show every extreme that they name: `seq_lengths`: tokens at positions below a sequence's length are real and later ones are padding; some sequence fills all 1536 slots in every draw.
All inputs are finite; a program needn't handle non-finite values.
Results may differ from the reference program's by a relative error of at most 0.02.
Values may be sent and summed in bfloat16 or wider, within the bound.
No kernel may reach another device: no remote copies, remote signals or barrier semaphores. Data moves between devices by JAX's collectives and lax.ppermute only.
A program may use at most 320 MiB of HBM per device.

```python
import jax
import jax.numpy as jnp
from jax import lax

D = 1152
HEADS = 4
HEAD_DIM = 256
FF = 6912
WINDOW = 512
SLOTS = 192
MICRO = 2
QW = 1024
GAINS = 5120
SEQS = 4
MICRO_TOKENS = 768
SEQ_LEN = 1536


def draw_seq_lengths(key, part):
    draw_key, pick_key = jax.random.split(key)
    lengths = jax.random.randint(draw_key, (SEQS,), SEQ_LEN // 2, SEQ_LEN + 1)
    full_index = jax.random.randint(pick_key, (), 0, SEQS)
    return jnp.where(jnp.arange(SEQS) == full_index, SEQ_LEN, lengths).astype(jnp.int32)


def with_spikes(array, stream_key, source, target, parts, factor):
    owner, partner = [(jnp.arange(array.shape[position]) // (array.shape[position] // parts)).reshape([-1 if axis == position else 1 for axis in range(array.ndim)]) for position in (source, target)]
    chosen = jax.random.permutation(stream_key, parts)[partner]
    strong = (owner == chosen) | (owner == (partner + parts // 2) % parts)
    return jnp.where(strong, factor * array, array)


def shard_levels(stream_key, dims, shards, least, largest):
    def one(axis_at, parts):
        steps = jax.random.uniform(jax.random.fold_in(jax.random.fold_in(stream_key, 6), axis_at), (parts,), jnp.float32, least / len(shards), largest / len(shards))
        return jnp.repeat(jnp.exp(steps), dims[axis_at] // parts).reshape((-1,) + (1,) * (len(dims) - axis_at - 1))

    level = one(*shards[0])
    for cut in shards[1:]:
        level = level * one(*cut)
    return level


def centred(own_key, shape, deviation, limit, pieces=(), kind=jnp.bfloat16):
    values = jax.random.normal(own_key, shape, jnp.float32) * deviation
    if len(pieces) > 0:
        values = shard_levels(own_key, shape, pieces, -0.22, 0.18) * values
    return jnp.clip(values, min=-limit, max=limit).astype(kind)


def gaussian_with(stream_key, dims, scale, reach, cuts, heavy, held_as=jnp.bfloat16):
    drawn = scale * jax.random.normal(stream_key, dims, jnp.float32)
    if cuts:
        drawn = drawn * shard_levels(stream_key, dims, cuts, -0.22, 0.18)
    return jnp.clip(with_spikes(drawn, jax.random.fold_in(stream_key, 3), *heavy), -reach, reach).astype(held_as)


def setup_inputs(seed: int = 0) -> dict:
    seeds = jax.random.split(jax.random.key(seed), 9)
    boundary = gaussian_with(seeds[0], (2, SEQS, MICRO, MICRO_TOKENS, D), 1.0, 6.0, ((0, 2), (1, 4), (3, 4)), (3, 4, 4, 2.0))
    seq_lengths = draw_seq_lengths(jax.random.fold_in(seeds[8], 71), 0)
    heads_weight = centred(seeds[2], (2, D, QW + 2 * HEAD_DIM), D ** -0.5, 0.1875, ((0, 2), (1, 4)))
    merge_weight = centred(seeds[3], (2, QW, D), QW ** -0.5, 0.1875, ((0, 2), (1, 4)))
    gate_weight = centred(seeds[4], (2, D, FF), D ** -0.5, 0.1875, ((0, 2), (2, 4)))
    up_weight = centred(seeds[5], (2, D, FF), D ** -0.5, 0.1875, ((0, 2), (2, 4)))
    down_weight = centred(seeds[6], (2, FF, D), FF ** -0.5, 0.078125, ((0, 2), (1, 4)))
    norm_gains = jnp.clip(1.0 + 0.1 * jax.random.normal(seeds[7], (2, GAINS), jnp.float32), 0.5, 1.5)
    return {"boundary": boundary, "seq_lengths": seq_lengths, "heads_weight": heads_weight, "merge_weight": merge_weight, "gate_weight": gate_weight, "up_weight": up_weight, "down_weight": down_weight, "norm_gains": norm_gains}


EPSILON = 1e-06
MASKED = -1e+30
PRECISE = lax.Precision.HIGHEST

@jax.custom_vjp
def low(v):
    return lax.optimization_barrier(v.astype(jnp.bfloat16)).astype(jnp.float32)

@jax.custom_vjp
def low_back(v):
    return v

def low_keep(v):
    return (low(v), None)

def low_pass(kept, grad):
    return (grad,)

def back_keep(v):
    return (v, None)

def back_low(kept, grad):
    return (low(grad),)
low.defvjp(low_keep, low_pass)
low_back.defvjp(back_keep, back_low)

def normalize(values, factor):
    return values * lax.rsqrt(lax.optimization_barrier(jnp.mean(values * values, axis=-1, keepdims=True)) + EPSILON) * factor

def rotate(values, cosine_table, sine_table):
    half_dim = values.shape[-1] // 2
    lower_half = values[..., :half_dim]
    upper_half = values[..., half_dim:]
    return jnp.concatenate([lower_half * cosine_table - upper_half * sine_table, upper_half * cosine_table + lower_half * sine_table], axis=-1)

def rotary_tables(positions, head_dim):
    frequency = jnp.power(10000.0, jnp.arange(head_dim // 2, dtype=jnp.float32) * (-2.0 / head_dim))
    angles = positions.astype(jnp.float32)[:, None] * frequency[None, :]
    return (jnp.cos(angles), jnp.sin(angles))

def product(left, right):
    return jnp.dot(left, right, precision=PRECISE, preferred_element_type=jnp.float32)

def gating(gate_part, up_part):
    return jax.nn.gelu(gate_part, approximate=True) * up_part

def attend(query_low, key_low, value_low):
    seq_total = query_low.shape[0]
    front_pad = jnp.zeros((WINDOW, HEAD_DIM), jnp.float32)
    padded_keys = jnp.concatenate([front_pad, key_low], axis=0)
    padded_values = jnp.concatenate([front_pad, value_low], axis=0)
    query_blocks = query_low.reshape(seq_total // SLOTS, SLOTS, HEADS, HEAD_DIM)
    block_starts = jnp.arange(seq_total // SLOTS, dtype=jnp.int32) * SLOTS

    def attend_block(operands):
        query_block, block_start = operands
        key_rows = lax.dynamic_slice_in_dim(padded_keys, block_start, WINDOW + SLOTS, 0)
        value_rows = lax.dynamic_slice_in_dim(padded_values, block_start, WINDOW + SLOTS, 0)
        query_places = block_start + jnp.arange(SLOTS, dtype=jnp.int32)
        key_places = block_start - WINDOW + jnp.arange(WINDOW + SLOTS, dtype=jnp.int32)
        distance = query_places[:, None] - key_places[None, :]
        allowed = (key_places[None, :] >= 0) & (distance >= 0) & (distance < WINDOW)
        scores = low_back(jnp.einsum('phe,ke->hpk', query_block, key_rows, precision=PRECISE) * HEAD_DIM ** (-0.5))
        masked = jnp.where(allowed[None], scores, MASKED)
        row_max = lax.optimization_barrier(jnp.max(masked, axis=-1, keepdims=True))
        exponents = jnp.exp(masked - row_max)
        softmax_low = low(exponents / lax.optimization_barrier(jnp.sum(exponents, axis=-1, keepdims=True)))
        mixed = jnp.einsum('hpk,ke->phe', softmax_low, value_rows, precision=PRECISE)
        return low(low_back(mixed))
    mixed_all = lax.map(jax.checkpoint(attend_block), (query_blocks, block_starts))
    return mixed_all.reshape(seq_total, HEADS * HEAD_DIM)

def apply_layer(layer_in, length, layer_params):
    heads_matrix, merge_matrix, gate_matrix, up_matrix, down_matrix, gain_vector = layer_params
    gain_one = gain_vector[0:D]
    gain_two = gain_vector[D:2 * D]
    gain_three = gain_vector[2 * D:3 * D]
    gain_four = gain_vector[3 * D:4 * D]
    gain_query = gain_vector[4 * D:4 * D + HEAD_DIM]
    gain_key = gain_vector[4 * D + HEAD_DIM:4 * D + 2 * HEAD_DIM]
    positions = jnp.arange(SEQ_LEN, dtype=jnp.int32)
    valid = (positions < length).astype(jnp.float32)
    cosine_table, sine_table = rotary_tables(positions, HEAD_DIM)
    normed_low = low(normalize(layer_in, gain_one))
    projected = low_back(product(normed_low, heads_matrix))
    query = projected[:, :QW].reshape(SEQ_LEN, HEADS, HEAD_DIM)
    key_raw = projected[:, QW:QW + HEAD_DIM]
    value_raw = projected[:, QW + HEAD_DIM:]
    query_low = low(rotate(normalize(query, gain_query), cosine_table[:, None, :], sine_table[:, None, :]))
    key_low = low(rotate(normalize(key_raw, gain_key), cosine_table, sine_table))
    value_low = low(value_raw)
    mixed_low = attend(query_low, key_low, value_low)
    attended = low_back(product(mixed_low, merge_matrix))
    first_sum = layer_in + normalize(attended, gain_two)
    second_low = low(normalize(first_sum, gain_three))
    gate_value = low_back(product(second_low, gate_matrix))
    up_value = low_back(product(second_low, up_matrix))
    gated = low(gating(gate_value, up_value))
    branch = low_back(product(gated, down_matrix))
    return (first_sum + normalize(branch, gain_four)) * valid[:, None]

def reference(boundary, seq_lengths, heads_weight, merge_weight, gate_weight, up_weight, down_weight, norm_gains):
    inputs = boundary[0].astype(jnp.float32).reshape(SEQS, SEQ_LEN, D)
    cotangent = boundary[1].astype(jnp.float32).reshape(SEQS, SEQ_LEN, D)
    params = (heads_weight.astype(jnp.float32), merge_weight.astype(jnp.float32), gate_weight.astype(jnp.float32), up_weight.astype(jnp.float32), down_weight.astype(jnp.float32), norm_gains.astype(jnp.float32))
    probe_zeros = jnp.zeros((SEQS, SEQ_LEN, D), jnp.float32)

    def run_layer(layer_params, layer_inputs):

        def one_sequence(operands):
            sequence_in, length = operands
            return apply_layer(sequence_in, length, layer_params)
        return lax.map(jax.checkpoint(one_sequence), (layer_inputs, seq_lengths))

    def full_forward(layer_inputs, probe_add, all_params):
        layer_zero = tuple((stacked[0] for stacked in all_params))
        layer_one = tuple((stacked[1] for stacked in all_params))
        out_zero = run_layer(layer_zero, layer_inputs)
        middle = low(low_back(out_zero)) + probe_add
        out_one = run_layer(layer_one, middle)
        return (out_zero, out_one)
    (out_zero, out_one), pullback = jax.vjp(full_forward, inputs, probe_zeros, params)
    grad_inputs, grad_middle, grad_params = pullback((jnp.zeros_like(out_zero), cotangent))
    shape_out = (2, SEQS, MICRO, MICRO_TOKENS, D)
    activations = jnp.stack([out_zero, out_one]).reshape(shape_out).astype(jnp.bfloat16)
    boundary_grads = jnp.stack([grad_inputs, grad_middle]).reshape(shape_out).astype(jnp.bfloat16)
    return (activations, boundary_grads, grad_params[0], grad_params[1], grad_params[2], grad_params[3], grad_params[4], grad_params[5])
```

```python
import jax
import jax.numpy as jnp
from jax import lax
from jax.sharding import PartitionSpec as P

HEADS = 4
HEAD_DIM = 256
WINDOW = 512
EPSILON = 1e-06
MASKED = -1e30
F32 = jnp.float32
BF16 = jnp.bfloat16


def shifted(array, axis, by):
    length = lax.axis_size(axis)
    return lax.ppermute(array, axis, [(i, (i + by) % length) for i in range(length)])


def other_core(array):
    return lax.ppermute(array, "section", [(0, 1), (1, 0)])


def einsum(spec, *operands):
    return jnp.einsum(spec, *operands, preferred_element_type=F32)


def inverse_rms(values):
    return lax.rsqrt(jnp.mean(values * values, axis=-1, keepdims=True) + EPSILON)


def normalize(values, gain):
    return values * inverse_rms(values) * gain


def normalize_back(values, gain, grad):
    inverse = inverse_rms(values)
    unit = values * inverse
    scaled = grad * gain
    d_values = inverse * (scaled - unit * jnp.mean(scaled * unit, axis=-1, keepdims=True))
    d_gain = jnp.sum((grad * unit).reshape(-1, grad.shape[-1]), axis=0)
    return d_values, d_gain


def rotate(values, cosine, sine):
    half = values.shape[-1] // 2
    low, high = values[..., :half], values[..., half:]
    return jnp.concatenate([low * cosine - high * sine, high * cosine + low * sine], axis=-1)


def rotary_tables(positions):
    half = HEAD_DIM // 2
    frequency = jnp.power(10000.0, jnp.arange(half, dtype=F32) * (-2.0 / HEAD_DIM))
    angles = positions.astype(F32)[:, None] * frequency[None, :]
    return jnp.cos(angles), jnp.sin(angles)


def gating(gate, up):
    return jax.nn.gelu(gate, approximate=True) * up


def rows_of_all(rows):
    length = lax.axis_size("wshard")
    return jnp.concatenate([rows] + [shifted(rows, "wshard", d) for d in range(1, length)], axis=0)


def rows_to_owners(terms):
    length = lax.axis_size("wshard")
    count = terms.shape[0] // length
    total = terms[:count]
    for d in range(1, length):
        total = total + shifted(terms[d * count : (d + 1) * count].astype(BF16), "wshard", -d).astype(F32)
    return total


def layer_rows(shard, layer):
    length = lax.axis_size("wshard")
    count = shard.shape[0]
    parts = [shard]
    for d in range(1, length):
        route = [(layer * length + i, layer * length + (i + d) % length) for i in range(length)]
        parts.append(lax.ppermute(shard, ("section", "wshard"), route))
    ascending = jnp.concatenate(parts[::-1] * 2, axis=0)
    start = (length - 1 - lax.axis_index("wshard")) * count
    full = lax.dynamic_slice_in_dim(ascending, start, length * count, 0)
    received = lax.ppermute(full, "section", [(layer, 1 - layer)])
    return jnp.where(lax.axis_index("section") == layer, full, received)


def sum_over(array, axis):
    return jnp.sum(lax.all_to_all(array, axis, 0, 0, tiled=False).astype(F32), axis=0)


def local(
    boundary, seq_lengths, heads_weight, merge_weight, gate_weight, up_weight, down_weight, norm_gains
):
    core = lax.axis_index("section")
    first = core == 0
    seq_index = lax.axis_index("seq")
    seq_count = lax.axis_size("seq")
    shard_count = lax.axis_size("wshard")
    micro_count, slots, width = boundary.shape[2:]
    rows = slots // 2
    micro_tokens = seq_count * slots
    query_width = HEADS * HEAD_DIM
    hops = (WINDOW + slots - 1) // slots
    scale = HEAD_DIM**-0.5
    length = seq_lengths[0]

    both_gains = jnp.stack([norm_gains[0], other_core(norm_gains[0])])
    all_gains = jnp.where(first, both_gains, both_gains[::-1])
    gains = []
    for layer in range(2):
        vector = all_gains[layer]
        gains.append(
            [vector[k * width : (k + 1) * width] for k in range(4)]
            + [vector[4 * width + k * HEAD_DIM : 4 * width + (k + 1) * HEAD_DIM] for k in range(2)]
        )

    held = boundary[0, 0]
    swapped = other_core(jnp.where(first, held[:, rows:], held[:, :rows]))
    inputs = jnp.where(first, held[:, :rows], swapped)
    cotangents = jnp.where(first, swapped, held[:, rows:])

    heads_full = [layer_rows(heads_weight[0], 0), None]
    merge_full = [layer_rows(merge_weight[0], 0), None]
    ffn = [[], []]
    for weight in (gate_weight[0], up_weight[0], down_weight[0]):
        received = other_core(weight)
        ffn[0].append(jnp.where(first, weight, received))
        ffn[1].append(jnp.where(first, received, weight))

    token_at = jnp.arange(rows, dtype=jnp.int32)
    spans = []
    for micro in range(micro_count):
        base = micro * micro_tokens + seq_index * slots
        positions = base + core * rows + token_at
        key_positions = jnp.concatenate(
            [
                base - d * slots + side * rows + token_at
                for side in (core, 1 - core)
                for d in range(hops + 1)
            ]
        )
        distance = positions[:, None] - key_positions[None, :]
        allowed = (key_positions[None, :] >= 0) & (distance >= 0) & (distance < WINDOW)
        cosine, sine = rotary_tables(positions)
        valid = (positions < length).astype(F32)[:, None]
        spans.append((allowed, cosine, sine, valid))

    def attention_forward(layer, micro, layer_in, kept):
        gain = gains[layer]
        _, cosine, sine, _ = spans[micro]
        normed_low = normalize(layer_in, gain[0]).astype(BF16)
        projected = einsum("pd,dc->pc", normed_low, heads_full[layer])
        query = projected[:, :query_width].reshape(rows, HEADS, HEAD_DIM)
        query_low = rotate(normalize(query, gain[4]), cosine[:, None], sine[:, None]).astype(BF16)
        query_low = query_low.transpose(1, 0, 2).reshape(HEADS * rows, HEAD_DIM)
        key = projected[:, query_width : query_width + HEAD_DIM]
        key_low = rotate(normalize(key, gain[5]), cosine, sine).astype(BF16)
        value_low = projected[:, query_width + HEAD_DIM :].astype(BF16)
        own_pairs = jnp.concatenate([key_low, value_low], axis=1)
        mine = [own_pairs]
        for d in range(1, hops + 1):
            outgoing = jnp.where(seq_index >= seq_count - d, kept, own_pairs)
            mine.append(shifted(outgoing, "seq", d))
        mine = jnp.concatenate(mine, axis=0)
        pairs = jnp.concatenate([mine, other_core(mine)], axis=0)
        return normed_low, projected, query_low, pairs, own_pairs

    def probabilities(micro, query_low, pairs):
        allowed = spans[micro][0]
        scores = einsum("qe,ke->qk", query_low, pairs[:, :HEAD_DIM]) * scale
        scores = jnp.where(allowed[None], scores.reshape(HEADS, rows, -1), MASKED)
        row_max = jnp.max(scores, axis=-1, keepdims=True)
        exponents = jnp.exp(scores - row_max)
        prob = exponents / jnp.sum(exponents, axis=-1, keepdims=True)
        return prob.reshape(HEADS * rows, -1)

    def attention_mix(layer, micro, layer_in, query_low, pairs):
        prob = probabilities(micro, query_low, pairs)
        mixed = einsum("qk,ke->qe", prob.astype(BF16), pairs[:, HEAD_DIM:])
        mixed_low = mixed.astype(BF16).reshape(HEADS, rows, HEAD_DIM)
        mixed_low = mixed_low.transpose(1, 0, 2).reshape(rows, query_width)
        attended = einsum("pq,qd->pd", mixed_low, merge_full[layer])
        first_sum = layer_in + normalize(attended, gains[layer][1])
        second_low = normalize(first_sum, gains[layer][2]).astype(BF16)
        return prob, mixed_low, attended, first_sum, second_low

    def feed_forward(layer, second_all):
        gate_matrix, up_matrix, down_matrix = ffn[layer]
        gate = einsum("pd,df->pf", second_all, gate_matrix)
        up = einsum("pd,df->pf", second_all, up_matrix)
        gated = gating(gate, up).astype(BF16)
        return gate, up, gated, einsum("pf,fd->pd", gated, down_matrix)

    stores = {}
    results = {}
    layer_ins = [inputs[micro] for micro in range(micro_count)]
    for layer in range(2):
        if layer == 1:
            shards = lax.optimization_barrier((heads_weight[0], merge_weight[0], stores[0, 0][1]))
            heads_full[1] = layer_rows(shards[0], 1)
            merge_full[1] = layer_rows(shards[1], 1)
        kept = jnp.zeros((rows, 2 * HEAD_DIM), BF16)
        for micro in range(micro_count):
            layer_in = layer_ins[micro].astype(F32)
            normed_low, projected, query_low, pairs, kept = attention_forward(layer, micro, layer_in, kept)
            prob, mixed_low, attended, first_sum, second_low = attention_mix(
                layer, micro, layer_in, query_low, pairs
            )
            second_all = rows_of_all(second_low)
            gate, up, gated, terms = feed_forward(layer, second_all)
            branch = rows_to_owners(terms)
            out = (first_sum + normalize(branch, gains[layer][3])) * spans[micro][3]
            results[layer, micro] = out.astype(BF16)
            stores[layer, micro] = (
                layer_in, normed_low, projected, query_low, pairs, prob, mixed_low, attended,
                first_sum, second_all, gate, up, gated, branch,
            )
        layer_ins = [results[layer, micro] for micro in range(micro_count)]

    input_grads = {}
    heads_terms, merge_terms, gain_terms, ffn_terms = [], [], [], []
    grads = [cotangents[micro] for micro in range(micro_count)]
    for layer in (1, 0):
        gain = gains[layer]
        gate_matrix, up_matrix, down_matrix = ffn[layer]
        carry = jnp.zeros((rows, 2 * HEAD_DIM), F32)
        gathered = {}
        sums = None
        for micro in range(micro_count - 1, -1, -1):
            (
                layer_in, normed_low, projected, query_low, pairs, prob, mixed_low, attended,
                first_sum, second_all, gate, up, gated, branch,
            ) = stores[layer, micro]
            _, cosine, sine, valid = spans[micro]
            d_out = grads[micro].astype(F32) * valid
            d_branch, d_gain_four = normalize_back(branch, gain[3], d_out)
            branch_all = rows_of_all(d_branch.astype(BF16))
            d_gated = einsum("pd,fd->pf", branch_all, down_matrix)
            d_gate, d_up = jax.vjp(gating, gate, up)[1](d_gated)
            gate_low, up_low = d_gate.astype(BF16), d_up.astype(BF16)
            d_second = rows_to_owners(
                einsum("pf,df->pd", gate_low, gate_matrix) + einsum("pf,df->pd", up_low, up_matrix)
            )
            gathered[micro] = (second_all, branch_all, gate_low, up_low, gated)
            d_first_part, d_gain_three = normalize_back(first_sum, gain[2], d_second)
            d_first = d_out + d_first_part
            d_attended, d_gain_two = normalize_back(attended, gain[1], d_first)
            attended_low = d_attended.astype(BF16)
            merge_term = einsum("pq,pd->qd", mixed_low, attended_low)
            d_mixed = einsum("pd,qd->pq", attended_low, merge_full[layer]).astype(BF16)
            d_mixed = d_mixed.reshape(rows, HEADS, HEAD_DIM).transpose(1, 0, 2)
            d_mixed = d_mixed.reshape(HEADS * rows, HEAD_DIM)
            d_values = einsum("qk,qe->ke", prob.astype(BF16), d_mixed)
            d_prob = einsum("qe,ke->qk", d_mixed, pairs[:, HEAD_DIM:])
            d_scores = prob * (d_prob - jnp.sum(d_prob * prob, axis=-1, keepdims=True))
            d_scores = d_scores.astype(BF16)
            d_query = einsum("qk,ke->qe", d_scores, pairs[:, :HEAD_DIM]) * scale
            d_query = d_query.reshape(HEADS, rows, HEAD_DIM).transpose(1, 0, 2)
            d_keys = einsum("qk,qe->ke", d_scores, query_low) * scale
            d_pairs = jnp.concatenate([d_keys, d_values], axis=1)
            side_rows = (hops + 1) * rows
            d_mine = d_pairs[:side_rows] + other_core(d_pairs[side_rows:].astype(BF16)).astype(F32)
            own_grad = d_mine[:rows] + carry
            carry = jnp.zeros_like(carry)
            for d in range(1, hops + 1):
                returned = shifted(d_mine[d * rows : (d + 1) * rows].astype(BF16), "seq", -d).astype(F32)
                goes_back = seq_index >= seq_count - d
                own_grad = own_grad + jnp.where(goes_back, 0.0, returned)
                carry = carry + jnp.where(goes_back, returned, 0.0)
            query = projected[:, :query_width].reshape(rows, HEADS, HEAD_DIM)
            d_query_raw, d_gain_query = normalize_back(
                query, gain[4], rotate(d_query, cosine[:, None], -sine[:, None])
            )
            d_key_raw, d_gain_key = normalize_back(
                projected[:, query_width : query_width + HEAD_DIM],
                gain[5],
                rotate(own_grad[:, :HEAD_DIM], cosine, -sine),
            )
            d_projected = jnp.concatenate(
                [d_query_raw.reshape(rows, query_width), d_key_raw, own_grad[:, HEAD_DIM:]], axis=1
            ).astype(BF16)
            heads_term = einsum("pd,pc->dc", normed_low, d_projected)
            d_normed = einsum("pc,dc->pd", d_projected, heads_full[layer])
            d_input_part, d_gain_one = normalize_back(layer_in, gain[0], d_normed)
            input_grads[layer, micro] = (d_first + d_input_part).astype(BF16)
            gain_term = jnp.concatenate(
                [d_gain_one, d_gain_two, d_gain_three, d_gain_four, d_gain_query, d_gain_key]
            )
            terms = (heads_term, merge_term, gain_term)
            sums = terms if sums is None else jax.tree.map(jnp.add, sums, terms)
        grads = [input_grads[layer, micro] for micro in range(micro_count)]
        second_rows, branch_rows, gate_rows, up_rows, gated_rows = (
            jnp.concatenate([gathered[micro][k] for micro in range(micro_count)], axis=0) for k in range(5)
        )
        ffn_terms.append(
            jnp.stack(
                [
                    einsum("pd,pf->df", second_rows, gate_rows),
                    einsum("pd,pf->df", second_rows, up_rows),
                    einsum("pd,pf->df", branch_rows, gated_rows),
                ]
            )
        )
        heads_terms.append(sums[0])
        merge_terms.append(sums[1])
        gain_terms.append(sums[2])

    def at_layer_core(terms):
        own = jnp.where(first, terms[1], terms[0])
        other = jnp.where(first, terms[0], terms[1])
        return own + other_core(other.astype(BF16)).astype(F32)

    def summed_rows(terms):
        total = at_layer_core(terms).astype(BF16)
        block = total.shape[0] // seq_count
        total = sum_over(total.reshape(seq_count, block, -1), "seq").astype(BF16)
        return sum_over(total.reshape(shard_count, block // shard_count, -1), "wshard")

    heads_gradient = summed_rows(heads_terms)
    merge_gradient = summed_rows(merge_terms)
    gains_gradient = summed_rows([term[:, None] for term in gain_terms])[:, 0]

    total = at_layer_core(ffn_terms).astype(BF16)
    hidden = total.shape[2]
    piece = width // seq_count
    groups = seq_count // shard_count
    block = hidden // seq_count
    total = total.reshape(3, seq_count, piece, hidden).transpose(1, 0, 2, 3)
    total = sum_over(total, "seq").astype(BF16)
    total = total.reshape(3, piece, groups, shard_count, block).transpose(3, 2, 0, 1, 4)
    total = lax.all_to_all(total, "wshard", 0, 0, tiled=False)
    total = total.reshape(seq_count, 3, piece, block)
    total = lax.all_to_all(total, "seq", 0, 0, tiled=False)
    total = total.transpose(1, 0, 2, 3).reshape(3, width, block).astype(F32)

    def at_sections(pieces):
        stacked = [jnp.stack(pieces[layer]) for layer in range(2)]
        received = other_core(jnp.where(first, stacked[1], stacked[0]))
        own = jnp.where(first, stacked[0], stacked[1])
        lower = jnp.where(first, own, received)
        upper = jnp.where(first, received, own)
        return jnp.concatenate([lower, upper], axis=1)[None, None]

    activations = at_sections([[results[layer, m] for m in range(micro_count)] for layer in range(2)])
    boundary_grads = at_sections([[input_grads[layer, m] for m in range(micro_count)] for layer in range(2)])
    return (
        activations,
        boundary_grads,
        heads_gradient[None],
        merge_gradient[None],
        total[0][None],
        total[1][None],
        total[2].T[None],
        gains_gradient[None],
    )


def solution(mesh):
    placed = (
        P("section", "wshard", None, "seq", None),
        P("wshard"),
        P("section", "wshard", None),
        P("section", "wshard", None),
        P("section", None, "wshard"),
        P("section", None, "wshard"),
        P("section", "wshard", None),
        P("section", None),
    )
    return jax.shard_map(
        local,
        mesh=mesh,
        in_specs=placed,
        out_specs=(
            P("section", "wshard", None, "seq", None),
            P("section", "wshard", None, "seq", None),
            P("section", ("seq", "wshard"), None),
            P("section", ("seq", "wshard"), None),
            P("section", None, ("seq", "wshard")),
            P("section", None, ("seq", "wshard")),
            P("section", ("seq", "wshard"), None),
            P("section", ("seq", "wshard")),
        ),
        check_vma=False,
    )
```

```python
import functools

import jax
import jax.numpy as jnp
from jax import lax
from jax.experimental import pallas as pl
from jax.experimental.pallas import tpu as pltpu
from jax.sharding import PartitionSpec as P


HEADS = 4
HEAD_DIM = 256
WINDOW = 512
EPSILON = 1e-06
MASKED = -1e30
F32 = jnp.float32
BF16 = jnp.bfloat16


def shifted(array, axis, by):
    length = lax.axis_size(axis)
    return lax.ppermute(array, axis, [(i, (i + by) % length) for i in range(length)])


def other_core(array):
    return lax.ppermute(array, "section", [(0, 1), (1, 0)])


def hop(array, by, flip):
    length = lax.axis_size("seq")
    route = [
        (core * length + i, (core ^ flip) * length + (i + by) % length)
        for core in range(2)
        for i in range(length)
    ]
    return lax.ppermute(array, ("section", "seq"), route)


def einsum(spec, *operands):
    return jnp.einsum(spec, *operands, preferred_element_type=F32)


def inverse_rms(values):
    return lax.rsqrt(jnp.mean(values * values, axis=-1, keepdims=True) + EPSILON)


def normalize(values, gain):
    return values * inverse_rms(values) * gain


def normalize_back(values, gain, grad):
    inverse = inverse_rms(values)
    unit = values * inverse
    scaled = grad * gain
    d_values = inverse * (scaled - unit * jnp.mean(scaled * unit, axis=-1, keepdims=True))
    return d_values, jnp.sum(grad * unit, axis=0, keepdims=True)


def rotary_tables(positions):
    half = HEAD_DIM // 2
    frequency = jnp.power(10000.0, jnp.arange(half, dtype=F32) * (-2.0 / HEAD_DIM))
    angles = positions.astype(F32)[:, None] * frequency[None, :]
    return jnp.cos(angles), jnp.sin(angles)


def sum_over(array, axis):
    return jnp.sum(lax.all_to_all(array, axis, 0, 0, tiled=False).astype(F32), axis=0)


def call(body, outs, operands, scalars=None, in_hbm=(), scratch=(), flops=0, vmem=24, name=None):
    specs = [pl.BlockSpec(memory_space=pltpu.SMEM)] if scalars is not None else []
    specs += [
        pl.BlockSpec(memory_space=pl.ANY if k in in_hbm else pltpu.VMEM) for k in range(len(operands))
    ]
    given = ([scalars] if scalars is not None else []) + list(operands)
    shapes = [jax.ShapeDtypeStruct(shape, kind) for shape, kind in outs]
    moved = sum(a.size * a.dtype.itemsize for a in operands) // (2 if in_hbm else 1)
    moved += sum(s.size * s.dtype.itemsize for s in shapes)
    return pl.pallas_call(
        body,
        out_shape=shapes,
        in_specs=specs,
        out_specs=[pl.BlockSpec(memory_space=pltpu.VMEM)] * len(shapes),
        scratch_shapes=list(scratch),
        compiler_params=pltpu.CompilerParams(vmem_limit_bytes=vmem * 1024 * 1024),
        cost_estimate=pl.CostEstimate(flops=flops, bytes_accessed=moved, transcendentals=0),
        name=name,
    )(*given)


def dot(left, right):
    return lax.dot_general(left, right, (((1,), (0,)), ((), ())), preferred_element_type=F32)


def dot_nt(left, right):
    return lax.dot_general(left, right, (((1,), (1,)), ((), ())), preferred_element_type=F32)


def dot_tn(left, right):
    return lax.dot_general(left, right, (((0,), (0,)), ((), ())), preferred_element_type=F32)


def rotate(values, cosine, sine):
    half = values.shape[-1] // 2
    low, high = values[:, :half], values[:, half:]
    return jnp.concatenate([low * cosine - high * sine, high * cosine + low * sine], axis=1)


def project_kernel(hops, layer, meta, x, own, got, gain_one, gain_query, gain_key, cosine, sine, kept, *outs):
    normed_low, projected, query_low, own_pairs = outs[:4]
    heads, sem = outs[-2:]
    wait = load_matrix(meta, layer, own, got, heads, sem)
    rows = x.shape[0]
    cos, sin = cosine[...], sine[...]
    normed = normalize(x[...].astype(F32), gain_one[...]).astype(BF16)
    normed_low[...] = normed
    wait()
    product = dot(normed, heads[...])
    projected[...] = product
    for h in range(HEADS):
        query = normalize(product[:, h * HEAD_DIM : (h + 1) * HEAD_DIM], gain_query[...])
        query_low[h * rows : (h + 1) * rows, :] = rotate(query, cos, sin).astype(BF16)
    at = HEADS * HEAD_DIM
    key = rotate(normalize(product[:, at : at + HEAD_DIM], gain_key[...]), cos, sin)
    pairs = jnp.concatenate([key, product[:, at + HEAD_DIM :]], axis=1).astype(BF16)
    own_pairs[...] = pairs
    for d in range(1, hops + 1):
        wraps = meta[SEQ_INDEX] >= meta[SEQ_COUNT] - d
        outs[3 + d][...] = jnp.where(wraps, kept[...].astype(F32), pairs.astype(F32)).astype(BF16)


def load_matrix(meta, layer, own, got, buffer, sem):
    mine = pltpu.make_async_copy(own, buffer, sem)
    theirs = pltpu.make_async_copy(got, buffer, sem)
    pl.when(meta[CORE] == layer)(mine.start)
    pl.when(meta[CORE] != layer)(theirs.start)
    return mine.wait


CORE, SEQ_INDEX, SEQ_COUNT, BASE, LENGTH, SLOTS, SHARD_INDEX = range(7)


def masked_bias(meta, rows, hops):
    blocks = 2 * (hops + 1)
    query_at = lax.broadcasted_iota(jnp.int32, (rows, blocks * rows), 0)
    column = lax.broadcasted_iota(jnp.int32, (1, blocks * rows), 1)
    core, base = meta[CORE], meta[BASE]
    offset = jnp.zeros_like(column)
    for k in range(blocks):
        side = core if k <= hops else 1 - core
        start = base + side * rows - (k % (hops + 1)) * meta[SLOTS] - k * rows
        offset = jnp.where(column >= k * rows, start, offset)
    key_position = column + offset
    distance = query_at + (base + core * rows) - key_position
    ok = (key_position >= 0) & (distance >= 0) & (distance < WINDOW)
    return jnp.where(ok, 0.0, MASKED)


def softmax(meta, query, keys, hops):
    rows = query.shape[0] // HEADS
    scores = dot_nt(query, keys) * HEAD_DIM**-0.5
    bias = masked_bias(meta, rows, hops)
    scores = scores + jnp.concatenate([bias] * HEADS, axis=0)
    exponents = jnp.exp(scores - jnp.max(scores, axis=1, keepdims=True))
    return exponents / jnp.sum(exponents, axis=1, keepdims=True)


def attend_kernel(hops, layer, meta, x, query_low, own, got, gain_two, gain_three, *refs):
    blocks = 2 * (hops + 1)
    pair_refs = refs[:blocks]
    mixed_low, attended, first_sum, second_low, pairs, merge, sem = refs[blocks:]
    wait = load_matrix(meta, layer, own, got, merge, sem)
    rows = x.shape[0]
    for k, ref in enumerate(pair_refs):
        pairs[k * rows : (k + 1) * rows, :] = ref[...]
    prob = softmax(meta, query_low[...], pairs[:, :HEAD_DIM], hops)
    mixed = dot(prob.astype(BF16), pairs[:, HEAD_DIM:]).astype(BF16)
    mixed = jnp.concatenate([mixed[h * rows : (h + 1) * rows] for h in range(HEADS)], axis=1)
    mixed_low[...] = mixed
    wait()
    out = dot(mixed, merge[...])
    attended[...] = out
    total = x[...].astype(F32) + normalize(out, gain_two[...])
    first_sum[...] = total
    second_low[...] = normalize(total, gain_three[...]).astype(BF16)


def chunks_of(total, size):
    return [(at, min(size, total - at)) for at in range(0, total, size)]


CHUNK = 640


def load_weights(meta, layer, pairs, buffers, sems):
    waits = []
    for step, (at, size) in enumerate(chunks_of(buffers[0].shape[0], CHUNK)):
        waits.append(
            [
                load_matrix(
                    meta, layer, own.at[at : at + size], got.at[at : at + size],
                    buffer.at[at : at + size], sems.at[step, k],
                )
                for k, ((own, got), buffer) in enumerate(zip(pairs, buffers))
            ]
        )
    return waits


def return_parts(meta, total, terms, buffer):
    count, rows = len(terms), terms[0].shape[0]
    buffer[...] = total
    for k in range(count):
        block = lax.rem(meta[SHARD_INDEX] + (count - k), count)
        terms[k][...] = buffer[pl.ds(pl.multiple_of(block * rows, 8), rows), :].astype(BF16)


def feed_kernel(layer, parts, meta, rows_in, *refs):
    gate_own, gate_got, up_own, up_got, down_own, down_got = refs[:6]
    active, slope, gated = refs[6:9]
    terms = refs[9 : 9 + parts]
    gate_w, up_w, down_w, buffer, sems = refs[9 + parts :]
    waits = load_weights(
        meta, layer, ((gate_own, gate_got), (up_own, up_got), (down_own, down_got)), (gate_w, up_w, down_w), sems
    )
    x = rows_in[...]
    total = None
    for (at, size), (gate_wait, up_wait, down_wait) in zip(chunks_of(gate_w.shape[0], CHUNK), waits):
        gate_wait()
        v = dot_nt(x, gate_w[at : at + size, :])
        up_wait()
        u = dot_nt(x, up_w[at : at + size, :])
        k = (2.0 / jnp.pi) ** 0.5
        square = v * v
        t = jnp.tanh(k * v * (1.0 + 0.044715 * square))
        half = 0.5 * (1.0 + t)
        act = v * half
        der = half + 0.5 * v * (1.0 - t * t) * (k * (1.0 + 3 * 0.044715 * square))
        active[:, at : at + size] = act.astype(BF16)
        slope[:, at : at + size] = (der * u).astype(BF16)
        hidden = (act * u).astype(BF16)
        gated[:, at : at + size] = hidden
        down_wait()
        part = dot(hidden, down_w[at : at + size, :])
        total = part if total is None else total + part
    return_parts(meta, total, terms, buffer)


def finish_kernel(parts, meta, first_sum, gain_four, *refs):
    out, branch = refs[parts:]
    rows = first_sum.shape[0]
    total = refs[0][...].astype(F32)
    for ref in refs[1:parts]:
        total = total + ref[...].astype(F32)
    branch[...] = total
    value = first_sum[...] + normalize(total, gain_four[...])
    at = lax.broadcasted_iota(jnp.int32, value.shape, 0) + (meta[BASE] + meta[CORE] * rows)
    out[...] = jnp.where(at < meta[LENGTH], value, 0.0).astype(BF16)


def branch_back_kernel(meta, grad, branch, gain_four, branch_low, d_gain):
    rows = grad.shape[0]
    at = lax.broadcasted_iota(jnp.int32, grad.shape, 0) + (meta[BASE] + meta[CORE] * rows)
    d_out = jnp.where(at < meta[LENGTH], grad[...].astype(F32), 0.0)
    d_branch, d_gain[...] = normalize_back(branch[...], gain_four[...], d_out)
    branch_low[...] = d_branch.astype(BF16)


def feed_back_kernel(layer, parts, meta, active, slope, rows_in, *refs):
    gate_own, gate_got, up_own, up_got, down_own, down_got = refs[:6]
    gate_low, up_low = refs[6:8]
    terms = refs[8 : 8 + parts]
    down_w, gate_w, up_w, buffer, sems = refs[8 + parts :]
    waits = load_weights(
        meta, layer, ((down_own, down_got), (gate_own, gate_got), (up_own, up_got)), (down_w, gate_w, up_w), sems
    )
    y = rows_in[...]
    total = None
    for (at, size), (down_wait, gate_wait, up_wait) in zip(chunks_of(gate_w.shape[0], CHUNK), waits):
        down_wait()
        d_gated = dot_nt(y, down_w[at : at + size, :])
        d_gate = (d_gated * slope[:, at : at + size].astype(F32)).astype(BF16)
        d_up = (d_gated * active[:, at : at + size].astype(F32)).astype(BF16)
        gate_low[:, at : at + size] = d_gate
        up_low[:, at : at + size] = d_up
        gate_wait()
        part = dot(d_gate, gate_w[at : at + size, :])
        up_wait()
        part = part + dot(d_up, up_w[at : at + size, :])
        total = part if total is None else total + part
    return_parts(meta, total, terms, buffer)


def attend_back_kernel(hops, parts, layer, meta, grad, first_sum, attended, query_low, projected, own, got, *refs):
    gain_two, gain_three, gain_query, cosine, sine = refs[:5]
    second_parts, refs = refs[5 : 5 + parts], refs[5 + parts :]
    blocks = 2 * (hops + 1)
    pair_refs, refs = refs[:blocks], refs[blocks:]
    d_first, attended_low, query_grad, own_grad = refs[:4]
    sent, refs = refs[4 : 4 + blocks - 1], refs[4 + blocks - 1 :]
    d_gain_two, d_gain_three, d_gain_query, pairs, merge, sem = refs
    wait = load_matrix(meta, layer, own, got, merge, sem)
    rows = grad.shape[0]
    at = lax.broadcasted_iota(jnp.int32, grad.shape, 0) + (meta[BASE] + meta[CORE] * rows)
    d_out = jnp.where(at < meta[LENGTH], grad[...].astype(F32), 0.0)
    d_second = second_parts[0][...].astype(F32)
    for ref in second_parts[1:]:
        d_second = d_second + ref[...].astype(F32)
    part, d_gain_three[...] = normalize_back(first_sum[...], gain_three[...], d_second)
    total = d_out + part
    d_first[...] = total
    d_attended, d_gain_two[...] = normalize_back(attended[...], gain_two[...], total)
    low = d_attended.astype(BF16)
    attended_low[...] = low
    wait()
    d_mixed = dot_nt(low, merge[...]).astype(BF16)
    d_mixed = jnp.concatenate([d_mixed[:, h * HEAD_DIM : (h + 1) * HEAD_DIM] for h in range(HEADS)], axis=0)
    for k, ref in enumerate(pair_refs):
        pairs[k * rows : (k + 1) * rows, :] = ref[...]
    query = query_low[...]
    prob = softmax(meta, query, pairs[:, :HEAD_DIM], hops)
    d_prob = dot_nt(d_mixed, pairs[:, HEAD_DIM:])
    d_scores = prob * (d_prob - jnp.sum(d_prob * prob, axis=1, keepdims=True))
    d_scores = d_scores.astype(BF16)
    d_values = dot_tn(prob.astype(BF16), d_mixed)
    d_keys = dot_tn(d_scores, query) * HEAD_DIM**-0.5
    d_pairs = jnp.concatenate([d_keys, d_values], axis=1)
    own_grad[...] = d_pairs[:rows]
    for k, ref in enumerate(sent):
        ref[...] = d_pairs[(k + 1) * rows : (k + 2) * rows].astype(BF16)
    d_query = dot(d_scores, pairs[:, :HEAD_DIM]) * HEAD_DIM**-0.5
    cos, sin = cosine[...], sine[...]
    gain_sum = jnp.zeros_like(d_gain_query[...])
    for h in range(HEADS):
        columns = slice(h * HEAD_DIM, (h + 1) * HEAD_DIM)
        turned = rotate(d_query[h * rows : (h + 1) * rows], cos, -sin)
        raw, d_gain = normalize_back(projected[:, columns], gain_query[...], turned)
        query_grad[:, columns] = raw.astype(BF16)
        gain_sum = gain_sum + d_gain
    d_gain_query[...] = gain_sum


def project_back_kernel(hops, layer, meta, x, projected, query_grad, d_first, own_grad, carry, own, got, *refs):
    gain_one, gain_key, cosine, sine = refs[:4]
    blocks = 2 * (hops + 1)
    returned, refs = refs[4 : 4 + blocks - 1], refs[4 + blocks - 1 :]
    projected_low, input_grad, next_carry, d_gain_one, d_gain_key, heads, sem = refs
    wait = load_matrix(meta, layer, own, got, heads, sem)
    total = own_grad[...] + carry[...]
    earlier = jnp.zeros_like(total)
    for k, ref in enumerate(returned):
        d = (k + 1) % (hops + 1)
        value = ref[...].astype(F32)
        if d == 0:
            total = total + value
        else:
            goes_back = meta[SEQ_INDEX] >= meta[SEQ_COUNT] - d
            total = total + jnp.where(goes_back, 0.0, value)
            earlier = earlier + jnp.where(goes_back, value, 0.0)
    next_carry[...] = earlier
    at = HEADS * HEAD_DIM
    turned = rotate(total[:, :HEAD_DIM], cosine[...], -sine[...])
    raw, d_gain_key[...] = normalize_back(projected[:, at : at + HEAD_DIM], gain_key[...], turned)
    low = jnp.concatenate(
        [query_grad[...], raw.astype(BF16), total[:, HEAD_DIM:].astype(BF16)], axis=1
    )
    projected_low[...] = low
    wait()
    d_normed = dot_nt(low, heads[...])
    part, d_gain_one[...] = normalize_back(x[...].astype(F32), gain_one[...], d_normed)
    input_grad[...] = (d_first[...] + part).astype(BF16)


def weight_grad_kernel(streams, count, block, meta, *refs):
    kept, sent, whole, sem = refs[-4:]
    for m in range((len(refs) - 4) // (2 * streams)):
        pairs = [refs[2 * (m * streams + k) : 2 * (m * streams + k) + 2] for k in range(streams)]
        for at, size in chunks_of(pairs[0][0].shape[1], CHUNK):
            total = None
            for left, right in pairs:
                part = dot_tn(left[:, at : at + size], right[...])
                total = part if total is None else total + part
            total = total.astype(BF16)
            for k in range(count):
                low, high = max(at, k * block), min(at + size, (k + 1) * block)
                if low < high:
                    to = m * block + low - k * block
                    whole[k, to : to + high - low, :] = total[low - at : high - at]
    used = (len(refs) - 4) // (2 * streams) * block
    if whole.shape[1] > used:
        for k in range(count):
            whole[k, used:, :] = jnp.zeros((whole.shape[1] - used, whole.shape[2]), BF16)
    piece = kept.shape[2]
    waits = []
    for half in range(2):
        for q in range(count):
            for k in range(count):
                source = whole.at[k, pl.ds((half * count + q) * piece, piece)]
                stay = pltpu.make_async_copy(source, kept.at[q, k], sem.at[half, q, k])
                leave = pltpu.make_async_copy(source, sent.at[q, k], sem.at[half, q, k])
                pl.when(meta[CORE] == half)(stay.start)
                pl.when(meta[CORE] != half)(leave.start)
                waits.append(stay.wait)
    for wait in waits:
        wait()


def join_kernel(*refs):
    for k, ref in enumerate(refs[:-1]):
        refs[-1][k] = ref[...]


def place_kernel(axis, meta, *refs):
    parts, (out, sems) = refs[:-2], refs[-2:]
    count, rows, columns = parts[0].shape
    waits = []
    for e, part in enumerate(parts):
        s = lax.rem(meta[SEQ_INDEX] + (len(parts) - e), len(parts))
        for d in range(count):
            w = lax.rem(meta[SHARD_INDEX] + (count - d), count)
            if axis == 1:
                at = (pl.ds(pl.multiple_of(w * rows, 16), rows), pl.ds(pl.multiple_of(s * columns, 128), columns))
            else:
                at = (pl.ds(pl.multiple_of((w * len(parts) + s) * rows, 16), rows), slice(None))
            copy = pltpu.make_async_copy(part.at[d], out.at[at], sems.at[e, d])
            copy.start()
            waits.append(copy.wait)
    for wait in waits:
        wait()


def matrix_of(shard, layer, axis, meta, after=()):
    seq_count, shard_count = lax.axis_size("seq"), lax.axis_size("wshard")
    size = shard.shape[axis] // seq_count
    if size % (128 if axis else 16):
        full = lax.all_gather(shard, "wshard", axis=0, tiled=True)
        return full, other_core(full)

    def moved(array, name, by):
        length = lax.axis_size(name)
        route = [(layer * length + i, layer * length + (i + by) % length) for i in range(length)]
        return lax.ppermute(array, ("section", name), route)

    own = lax.dynamic_slice_in_dim(shard, lax.axis_index("seq") * size, size, axis)
    parts = [own] + [moved(own, "wshard", d) for d in range(1, shard_count)]
    parts = lax.optimization_barrier(tuple(parts) + tuple(after))[:shard_count]
    joined = call(join_kernel, [((shard_count,) + own.shape, BF16)], parts, vmem=4)[0]
    parts = [joined] + [moved(joined, "seq", e) for e in range(1, seq_count)]
    full = (shard.shape[0] * shard_count, shard.shape[1])
    placed = call(
        functools.partial(place_kernel, axis),
        [(full, BF16)],
        parts,
        scalars=meta,
        in_hbm=range(seq_count),
        scratch=[pltpu.SemaphoreType.DMA((seq_count, shard_count))],
        vmem=8,
    )[0]
    received = lax.ppermute(placed, "section", [(layer, 1 - layer)])
    return placed, received


def local(
    boundary, seq_lengths, heads_weight, merge_weight, gate_weight, up_weight, down_weight, norm_gains
):
    core = lax.axis_index("section")
    first = core == 0
    seq_index = lax.axis_index("seq")
    seq_count = lax.axis_size("seq")
    shard_count = lax.axis_size("wshard")
    micro_count, slots, width = boundary.shape[2:]
    rows = slots // 2
    micro_tokens = seq_count * slots
    query_width = HEADS * HEAD_DIM
    head_columns = heads_weight.shape[2]
    hidden = gate_weight.shape[2]
    hops = (WINDOW + slots - 1) // slots
    blocks = 2 * (hops + 1)
    all_rows = shard_count * rows

    both_gains = jnp.stack([norm_gains[0], other_core(norm_gains[0])])
    all_gains = jnp.where(first, both_gains, both_gains[::-1])
    gains = []
    for layer in range(2):
        vector = all_gains[layer][None]
        gains.append(
            [vector[:, k * width : (k + 1) * width] for k in range(4)]
            + [vector[:, 4 * width + k * HEAD_DIM : 4 * width + (k + 1) * HEAD_DIM] for k in range(2)]
        )

    metas, tables = [], []
    for micro in range(micro_count):
        base = micro * micro_tokens + seq_index * slots
        entries = [core, seq_index, seq_count, base, seq_lengths[0], slots, lax.axis_index("wshard")]
        metas.append(jnp.stack([jnp.asarray(e, jnp.int32) for e in entries]))
        tables.append(rotary_tables(base + core * rows + jnp.arange(rows, dtype=jnp.int32)))

    held = boundary[0, 0]
    swapped = other_core(jnp.where(first, held[:, rows:], held[:, :rows]))
    inputs = jnp.where(first, held[:, :rows], swapped)
    cotangents = jnp.where(first, swapped, held[:, rows:])

    matrices = [None, None]

    def attention_matrices(layer, after):
        shards = (heads_weight[0], merge_weight[0])
        if after is not None:
            shards = lax.optimization_barrier(shards + (after,))[:2]
        received = [array for pair in ffn for array in pair[1:]] if after is None else []
        matrices[layer] = [
            matrix_of(shard, layer, axis, metas[0], received) for shard, axis in zip(shards, (1, 0))
        ]

    ffn = [(weight, other_core(weight)) for weight in (gate_weight[0].T, up_weight[0].T, down_weight[0])]
    ffn_operands = [array for pair in ffn for array in pair]
    weight_buffers = [pltpu.VMEM((hidden, width), BF16)] * 3 + [
        pltpu.VMEM((all_rows, width), F32),
        pltpu.SemaphoreType.DMA((len(chunks_of(hidden, CHUNK)), 3)),
    ]
    attention_matrices(0, None)

    def gather_rows(array):
        return lax.all_gather(array, "wshard", axis=0, tiled=True)

    def return_rows(parts):
        return [parts[0]] + [shifted(parts[d], "wshard", -d) for d in range(1, shard_count)]

    stores, results = {}, {}
    layer_ins = [inputs[micro] for micro in range(micro_count)]
    for layer in range(2):
        gain = gains[layer]
        kept = jnp.zeros((rows, 2 * HEAD_DIM), BF16)
        for micro in range(micro_count):
            meta, (cosine, sine), x = metas[micro], tables[micro], layer_ins[micro]
            heads, merge = matrices[layer]
            normed_low, projected, query_low, kept, *outgoing = call(
                functools.partial(project_kernel, hops, layer),
                [
                    ((rows, width), BF16),
                    ((rows, head_columns), F32),
                    ((HEADS * rows, HEAD_DIM), BF16),
                    ((rows, 2 * HEAD_DIM), BF16),
                ]
                + [((rows, 2 * HEAD_DIM), BF16)] * hops,
                [x, *heads, gain[0], gain[4], gain[5], cosine, sine, kept],
                scalars=meta,
                in_hbm=(1, 2),
                scratch=[pltpu.VMEM((width, head_columns), BF16), pltpu.SemaphoreType.DMA],
                vmem=16,
                flops=2 * rows * width * head_columns,
                name="project",
            )
            pairs = [kept] + [hop(outgoing[d - 1], d, 0) for d in range(1, hops + 1)]
            pairs += [hop(([kept] + outgoing)[d], d, 1) for d in range(hops + 1)]
            if layer == 0 and micro == 0:
                attention_matrices(1, kept)
            mixed_low, attended, first_sum, second_low = call(
                functools.partial(attend_kernel, hops, layer),
                [
                    ((rows, query_width), BF16),
                    ((rows, width), F32),
                    ((rows, width), F32),
                    ((rows, width), BF16),
                ],
                [x, query_low, *merge, gain[1], gain[2]] + pairs,
                scalars=meta,
                in_hbm=(2, 3),
                scratch=[
                    pltpu.VMEM((blocks * rows, 2 * HEAD_DIM), BF16),
                    pltpu.VMEM((query_width, width), BF16),
                    pltpu.SemaphoreType.DMA,
                ],
                vmem=20,
                flops=2 * rows * query_width * (width + 2 * blocks * rows),
                name="attend",
            )
            second_all = gather_rows(second_low)
            active, slope, gated, *parts = call(
                functools.partial(feed_kernel, layer, shard_count),
                [((all_rows, hidden), BF16)] * 3 + [((rows, width), BF16)] * shard_count,
                [second_all] + ffn_operands,
                scalars=meta,
                in_hbm=range(1, 7),
                scratch=weight_buffers,
                flops=6 * all_rows * width * hidden,
                vmem=36,
                name="feed",
            )
            out, branch = call(
                functools.partial(finish_kernel, shard_count),
                [((rows, width), BF16), ((rows, width), F32)],
                [first_sum, gain[3]] + return_rows(parts),
                scalars=meta,
                vmem=8,
                name="finish",
            )
            results[layer, micro] = out
            stores[layer, micro] = (
                x, normed_low, projected, query_low, pairs, mixed_low, attended,
                first_sum, second_all, active, slope, gated, branch,
            )
        layer_ins = [results[layer, micro] for micro in range(micro_count)]

    def halves_swapped(total, axis):
        size = total.shape[axis] // 2
        keep = lax.dynamic_slice_in_dim(total, core * size, size, axis)
        send = lax.dynamic_slice_in_dim(total, (1 - core) * size, size, axis)
        return (keep.astype(F32) + other_core(send).astype(F32)).astype(BF16)

    block = hidden // seq_count
    groups = seq_count // shard_count

    def ffn_gradient(pairs):
        matrix_count = len(pairs)
        piece = -(-matrix_count * block // (2 * seq_count * 16)) * 16
        if block % 16:
            whole = jnp.concatenate(
                [
                    sum(einsum("pf,pd->fd", *pair) for pair in matrix).astype(BF16).reshape(seq_count, block, width)
                    for matrix in pairs
                ],
                axis=1,
            )
            whole = jnp.pad(whole, ((0, 0), (0, 2 * seq_count * piece - matrix_count * block), (0, 0)))
            whole = whole.reshape(seq_count, 2, seq_count, piece, width).transpose(1, 2, 0, 3, 4)
            keep, send = (lax.dynamic_index_in_dim(whole, c, 0, False) for c in (core, 1 - core))
        else:
            given = [array for matrix in pairs for pair in matrix for array in pair]
            keep, send = pl.pallas_call(
                functools.partial(weight_grad_kernel, micro_count, seq_count, block),
                out_shape=[jax.ShapeDtypeStruct((seq_count, seq_count, piece, width), BF16)] * 2,
                in_specs=[pl.BlockSpec(memory_space=pltpu.SMEM)]
                + [pl.BlockSpec(memory_space=pltpu.VMEM)] * len(given),
                out_specs=[pl.BlockSpec(memory_space=pl.ANY)] * 2,
                scratch_shapes=[
                    pltpu.VMEM((seq_count, 2 * seq_count * piece, width), BF16),
                    pltpu.SemaphoreType.DMA((2, seq_count, seq_count)),
                ],
                compiler_params=pltpu.CompilerParams(vmem_limit_bytes=40 * 1024 * 1024),
                cost_estimate=pl.CostEstimate(
                    flops=2 * matrix_count * micro_count * all_rows * width * hidden,
                    bytes_accessed=matrix_count * width * hidden * 4,
                    transcendentals=0,
                ),
                name="weight_grad",
            )(metas[0], *given)
        return (keep.astype(F32) + other_core(send).astype(F32)).astype(BF16)

    def summed_pieces(total):
        return sum_over(total, "seq").astype(BF16)

    def owners_pieces(total):
        total = total.reshape((groups, shard_count) + total.shape[1:]).swapaxes(0, 1)
        total = lax.all_to_all(total, "wshard", 0, 0, tiled=False)
        return lax.all_to_all(total.reshape((seq_count,) + total.shape[2:]), "seq", 0, 0, tiled=False)

    def attention_gradient(terms):
        normed, d_projected, mixed, d_attended = (
            jnp.concatenate([terms[micro][k] for micro in range(micro_count)]) for k in range(4)
        )
        heads = einsum("pd,pc->dc", normed, d_projected).astype(BF16)
        merge = einsum("pq,pd->qd", mixed, d_attended).astype(BF16)
        owners = seq_count * shard_count
        heads = halves_swapped(heads, 1)
        merge = halves_swapped(merge.reshape(owners, -1, width), 1)
        found = []
        for total in (heads, merge):
            total = sum_over(total.reshape(seq_count, -1, total.shape[-1]), "seq").astype(BF16)
            found.append(sum_over(total.reshape(shard_count, -1, total.shape[-1]), "wshard").astype(BF16))
        return found

    input_grads = {}
    ffn_shares, attention_shares, gain_sums = {}, {}, {}
    grads = [cotangents[micro] for micro in range(micro_count)]
    for layer in (1, 0):
        gain = gains[layer]
        heads, merge = matrices[layer]
        carry = jnp.zeros((rows, 2 * HEAD_DIM), F32)
        gathered, terms = {}, {}
        gain_sum = None
        for micro in range(micro_count - 1, -1, -1):
            (
                x, normed_low, projected, query_low, pairs, mixed_low, attended,
                first_sum, second_all, active, slope, gated, branch,
            ) = stores[layer, micro]
            meta, (cosine, sine) = metas[micro], tables[micro]
            grad = grads[micro]
            branch_low, d_gain_four = call(
                branch_back_kernel,
                [((rows, width), BF16), ((1, width), F32)],
                [grad, branch, gain[3]],
                scalars=meta,
                vmem=8,
                name="branch_back",
            )
            branch_all = gather_rows(branch_low)
            gate_low, up_low, *parts = call(
                functools.partial(feed_back_kernel, layer, shard_count),
                [((all_rows, hidden), BF16)] * 2 + [((rows, width), BF16)] * shard_count,
                [active, slope, branch_all] + ffn_operands,
                scalars=meta,
                in_hbm=range(3, 9),
                scratch=weight_buffers,
                flops=6 * all_rows * width * hidden,
                vmem=36,
                name="feed_back",
            )
            gathered[micro] = (second_all, branch_all, gate_low, up_low, gated)
            if micro == 0:
                order = range(micro_count)
                down = ffn_gradient([[(gathered[k][4], gathered[k][1]) for k in order]])
                others = ffn_gradient([[(gathered[k][j], gathered[k][0]) for k in order] for j in (2, 3)])
                ffn_shares[layer] = [down, others]
            parts = return_rows(parts)
            if layer == 0:
                if micro == micro_count - 1:
                    pending = [summed_pieces(total) for total in ffn_shares[1]]
                else:
                    pending = [owners_pieces(total) for total in ffn_shares[1]]
                parts, pending = lax.optimization_barrier((parts, pending))
                ffn_shares[1] = pending
            outs = call(
                functools.partial(attend_back_kernel, hops, shard_count, layer),
                [
                    ((rows, width), F32),
                    ((rows, width), BF16),
                    ((rows, query_width), BF16),
                    ((rows, 2 * HEAD_DIM), F32),
                ]
                + [((rows, 2 * HEAD_DIM), BF16)] * (blocks - 1)
                + [((1, width), F32), ((1, width), F32), ((1, HEAD_DIM), F32)],
                [grad, first_sum, attended, query_low, projected, *merge]
                + [gain[1], gain[2], gain[4], cosine, sine]
                + parts
                + pairs,
                scalars=meta,
                in_hbm=(5, 6),
                scratch=[
                    pltpu.VMEM((blocks * rows, 2 * HEAD_DIM), BF16),
                    pltpu.VMEM((query_width, width), BF16),
                    pltpu.SemaphoreType.DMA,
                ],
                vmem=28,
                flops=2 * rows * query_width * (width + 5 * blocks * rows),
                name="attend_back",
            )
            d_first, attended_low, query_grad, own_grad = outs[:4]
            returned = [hop(outs[3 + d], -d, 0) for d in range(1, hops + 1)]
            returned += [hop(outs[4 + hops + d], -d, 1) for d in range(hops + 1)]
            d_gain_two, d_gain_three, d_gain_query = outs[-3:]
            projected_low, input_grad, carry, d_gain_one, d_gain_key = call(
                functools.partial(project_back_kernel, hops, layer),
                [
                    ((rows, head_columns), BF16),
                    ((rows, width), BF16),
                    ((rows, 2 * HEAD_DIM), F32),
                    ((1, width), F32),
                    ((1, HEAD_DIM), F32),
                ],
                [x, projected, query_grad, d_first, own_grad, carry, *heads, gain[0], gain[5], cosine, sine]
                + returned,
                scalars=meta,
                in_hbm=(6, 7),
                scratch=[pltpu.VMEM((width, head_columns), BF16), pltpu.SemaphoreType.DMA],
                vmem=16,
                flops=2 * rows * width * head_columns,
                name="project_back",
            )
            input_grads[layer, micro] = input_grad
            terms[micro] = (normed_low, projected_low, mixed_low, attended_low)
            vector = jnp.concatenate(
                [d_gain_one, d_gain_two, d_gain_three, d_gain_four, d_gain_query, d_gain_key], axis=1
            )
            gain_sum = vector if gain_sum is None else gain_sum + vector
        grads = [input_grads[layer, micro] for micro in range(micro_count)]
        attention_shares[layer] = attention_gradient(terms)
        gain_sums[layer] = gain_sum

    def to_layer_core(shares):
        received = other_core(jnp.where(first, shares[1], shares[0]))
        own = jnp.where(first, shares[0], shares[1])
        return jnp.where(first, own, received), jnp.where(first, received, own)

    ffn_shares[0] = [owners_pieces(summed_pieces(total)) for total in ffn_shares[0]]
    own = jnp.where(first, gain_sums[0], gain_sums[1])
    other = jnp.where(first, gain_sums[1], gain_sums[0])
    total = own + other_core(other.astype(BF16)).astype(F32)
    total = sum_over(total.astype(BF16).reshape(seq_count, -1), "seq").astype(BF16)
    gains_gradient = sum_over(total.reshape(shard_count, -1), "wshard")

    heads_gradient = jnp.concatenate(to_layer_core({k: v[0] for k, v in attention_shares.items()}), axis=1)
    merge_gradient = jnp.concatenate(to_layer_core({k: v[1] for k, v in attention_shares.items()}), axis=0)
    def owned(index, count):
        done = {layer: ffn_shares[layer][index] for layer in range(2)}
        lower, upper = to_layer_core(done)
        share = jnp.concatenate([lower.reshape(-1, width), upper.reshape(-1, width)], axis=0).astype(F32)
        return [share[k * block : (k + 1) * block] for k in range(count)]

    (down_gradient,) = owned(0, 1)
    gate_gradient, up_gradient = owned(1, 2)

    def at_sections(pieces):
        stacked = [jnp.stack(pieces[layer]) for layer in range(2)]
        lower, upper = to_layer_core(stacked)
        return jnp.concatenate([lower, upper], axis=1)[None, None]

    activations = at_sections([[results[layer, m] for m in range(micro_count)] for layer in range(2)])
    boundary_grads = at_sections([[input_grads[layer, m] for m in range(micro_count)] for layer in range(2)])
    return (
        activations,
        boundary_grads,
        heads_gradient.astype(F32)[None],
        merge_gradient.astype(F32)[None],
        gate_gradient.T[None],
        up_gradient.T[None],
        down_gradient[None],
        gains_gradient[None],
    )


def solution(mesh):
    placed = (
        P("section", "wshard", None, "seq", None),
        P("wshard"),
        P("section", "wshard", None),
        P("section", "wshard", None),
        P("section", None, "wshard"),
        P("section", None, "wshard"),
        P("section", "wshard", None),
        P("section", None),
    )
    return jax.shard_map(
        local,
        mesh=mesh,
        in_specs=placed,
        out_specs=(
            P("section", "wshard", None, "seq", None),
            P("section", "wshard", None, "seq", None),
            P("section", ("seq", "wshard"), None),
            P("section", ("seq", "wshard"), None),
            P("section", None, ("seq", "wshard")),
            P("section", None, ("seq", "wshard")),
            P("section", ("seq", "wshard"), None),
            P("section", ("seq", "wshard")),
        ),
        check_vma=False,
    )
```
